32 devices in a mesh: dp: 2 (over y), rows: 4 (over x, core), cols: 4 (over z).
Axes of the slice: x: 2, y: 2, z: 4, core: 2. Of those that a mesh axis runs over, the one named last changes fastest.
Arguments:
- tokens: bfloat16 [960, 8192], P('rows', ('dp', 'cols')), may hold values from -6 to 6
- query_weight: bfloat16 [2, 960, 960], P(None, 'rows', 'cols'), may hold values from -0.1875 to 0.1875
- key_weight: bfloat16 [2, 960, 320], P(None, 'rows', 'cols'), may hold values from -0.1875 to 0.1875
- value_weight: bfloat16 [2, 960, 320], P(None, 'rows', 'cols'), may hold values from -0.1875 to 0.1875
- out_weight: bfloat16 [2, 960, 960], P(None, 'cols', 'rows'), may hold values from -1.25 to 1.25
- gate_weight: bfloat16 [2, 960, 2560], P(None, 'rows', 'cols'), may hold values from -0.1875 to 0.1875
- up_weight: bfloat16 [2, 960, 2560], P(None, 'rows', 'cols'), may hold values from -0.1875 to 0.1875
- down_weight: bfloat16 [2, 960, 2560], P(None, 'rows', 'cols'), may hold values from -0.125 to 0.125
- attention_gain: float32 [2, 960], replicated, may hold values from 0.5 to 1.5
- feedforward_gain: float32 [2, 960], replicated, may hold values from 0.5 to 1.5
- positions: int32 [8, 1024], P('dp'), may hold values from 0 to 2047, as said below
- segments: int32 [8, 1024], P('dp'), may hold values from 0 to 2, as said below
- cotangent: bfloat16 [960, 8192], P('rows', ('dp', 'cols')), may hold values from -6 to 6
Outputs:
- layer_out: float32 [960, 8192], P('rows', ('dp', 'cols'))
- input_grad: float32 [960, 8192], P('rows', ('dp', 'cols'))
- query_grad: float32 [2, 960, 960], P(None, 'rows', 'cols')
- key_grad: float32 [2, 960, 320], P(None, 'rows', 'cols')
- value_grad: float32 [2, 960, 320], P(None, 'rows', 'cols')
- out_grad: float32 [2, 960, 960], P(None, 'cols', 'rows')
- gate_grad: float32 [2, 960, 2560], P(None, 'rows', 'cols')
- up_grad: float32 [2, 960, 2560], P(None, 'rows', 'cols')
- down_grad: float32 [2, 960, 2560], P(None, 'rows', 'cols')
- attention_gain_grad: float32 [2, 960], replicated
- feedforward_gain_grad: float32 [2, 960], replicated
The draws below stay inside these ranges and needn't reach their ends.
Inputs may be any that keep to these rules, and one draw needn't show every extreme that they name: Along a sequence the segment numbers never fall, and every sequence holds three segments. `positions`: A position counts from its document's first token; a sequence's first document may have begun before the sequence.
All inputs are finite; a program needn't handle non-finite values.
Results may differ from the reference program's by a relative error of at most 0.03.
Values may be sent and summed in bfloat16 or wider, within the bound.
No kernel may reach another device: no remote copies, remote signals or barrier semaphores. Data moves between devices by JAX's collectives and lax.ppermute only.
A program may use at most 192 MiB of HBM per device.

```python
import jax
import jax.numpy as jnp
from jax import lax

D = 960
HEADS = 15
KV_HEADS = 5
HEAD = 64
FF = 2560
LAYERS = 2
SEQ = 1024
TOKENS = 8192
NSEQ = 8


def document_layout(key):
    inner_key = jax.random.fold_in(key, 31)
    first_key, second_key, offset_key = jax.random.split(inner_key, 3)
    first_cut = jax.random.randint(first_key, (NSEQ, 1), SEQ // 5, SEQ // 2)
    second_cut = first_cut + jax.random.randint(second_key, (NSEQ, 1), SEQ // 5, SEQ // 2)
    carried_top = 2 * SEQ - first_cut
    carried = jax.random.randint(offset_key, (NSEQ, 1), 0, carried_top + 1)
    seq_rows = jnp.arange(NSEQ, dtype=jnp.int32)[:, None]
    carried = jnp.where(seq_rows == 0, carried_top, carried)
    places = jnp.arange(SEQ, dtype=jnp.int32)[None, :]
    segment_ids = (places >= first_cut).astype(jnp.int32) + (places >= second_cut).astype(jnp.int32)
    doc_start = jnp.where(places >= second_cut, second_cut, jnp.where(places >= first_cut, first_cut, 0))
    position_ids = places - doc_start + jnp.where(places < first_cut, carried, 0)
    return (segment_ids, position_ids)


def draw_positions(key, part):
    return document_layout(key)[1]


def draw_segments(key, part):
    return document_layout(key)[0]


def shard_levels(own_key, dims, cuts, least, largest):
    def one(dim, blocks):
        steps = jax.random.uniform(jax.random.fold_in(jax.random.fold_in(own_key, 6), dim), (blocks,), jnp.float32, least / len(cuts), largest / len(cuts))
        return jnp.repeat(jnp.exp(steps), dims[dim] // blocks).reshape((-1,) + (1,) * (len(dims) - dim - 1))

    level = one(*cuts[0])
    for cut in cuts[1:]:
        level = level * one(*cut)
    return level


def centred(stream_key, extent, width, bound, cuts=(), kind=jnp.bfloat16):
    values = jax.random.normal(stream_key, extent, jnp.float32) * width
    if len(cuts) > 0:
        values = shard_levels(stream_key, extent, cuts, -0.22, 0.18) * values
    return jnp.clip(values, min=-bound, max=bound).astype(kind)


def setup_inputs(seed: int = 0) -> dict:
    splits = jax.random.split(jax.random.key(seed), 14)
    tokens = centred(splits[0], (D, TOKENS), 1.0, 6.0, ((0, 4), (1, 8)))
    query_weight = centred(splits[1], (LAYERS, D, HEADS * HEAD), D ** -0.5, 0.1875, ((1, 4), (2, 4)))
    key_weight = centred(splits[2], (LAYERS, D, KV_HEADS * HEAD), D ** -0.5, 0.1875, ((1, 4), (2, 4)))
    value_weight = centred(splits[3], (LAYERS, D, KV_HEADS * HEAD), D ** -0.5, 0.1875, ((1, 4), (2, 4)))
    out_weight = centred(splits[4], (LAYERS, HEADS * HEAD, D), (HEADS * HEAD // 40) ** -0.5, 1.25, ((1, 4), (2, 4)))
    gate_weight = centred(splits[5], (LAYERS, D, FF), D ** -0.5, 0.1875, ((1, 4), (2, 4)))
    up_weight = centred(splits[6], (LAYERS, D, FF), D ** -0.5, 0.1875, ((1, 4), (2, 4)))
    down_weight = centred(splits[7], (LAYERS, D, FF), FF ** -0.5, 0.125, ((1, 4), (2, 4)))
    attention_gain = jnp.clip(1.0 + 0.1 * jax.random.normal(splits[8], (LAYERS, D), jnp.float32), 0.5, 1.5)
    feedforward_gain = jnp.clip(1.0 + 0.1 * jax.random.normal(splits[9], (LAYERS, D), jnp.float32), 0.5, 1.5)
    positions = draw_positions(jax.random.fold_in(splits[13], 71), 0)
    segments = draw_segments(jax.random.fold_in(splits[13], 71), 0)
    cotangent = centred(splits[12], (D, TOKENS), 1.0, 6.0, ((0, 4), (1, 8)))
    return {"tokens": tokens, "query_weight": query_weight, "key_weight": key_weight, "value_weight": value_weight, "out_weight": out_weight, "gate_weight": gate_weight, "up_weight": up_weight, "down_weight": down_weight, "attention_gain": attention_gain, "feedforward_gain": feedforward_gain, "positions": positions, "segments": segments, "cotangent": cotangent}


EPSILON = 1e-05
NEG_FILL = -1e+30
ROPE_BASE = 100000.0
HIGHEST = lax.Precision.HIGHEST

@jax.custom_vjp
def low(v):
    return lax.optimization_barrier(v.astype(jnp.bfloat16)).astype(jnp.float32)

@jax.custom_vjp
def low_back(v):
    return v

def low_keep(v):
    return (low(v), None)

def low_pass(kept, grad):
    return (grad,)

def back_keep(v):
    return (v, None)

def back_low(kept, grad):
    return (low(grad),)
low.defvjp(low_keep, low_pass)
low_back.defvjp(back_keep, back_low)

def rope_tables(positions):
    half_dim = HEAD // 2
    frequency = ROPE_BASE ** (-2.0 * jnp.arange(half_dim, dtype=jnp.float32) / HEAD)
    phase_angle = positions.astype(jnp.float32)[:, None] * frequency[None, :]
    return (jnp.cos(phase_angle)[:, None, :], jnp.sin(phase_angle)[:, None, :])

def rotate(values, cosine, sine_part):
    half_dim = values.shape[-1] // 2
    lower_half = values[..., :half_dim]
    upper_half = values[..., half_dim:]
    return jnp.concatenate([lower_half * cosine - upper_half * sine_part, upper_half * cosine + lower_half * sine_part], -1)

def matmul_high(left, right):
    return jnp.dot(left, right, precision=HIGHEST)

def attend_sequence(items):
    queries, keys, values, segment_ids = items
    grouped = queries.reshape(SEQ, KV_HEADS, HEADS // KV_HEADS, HEAD)
    scores = low_back(jnp.einsum('qhgd,khd->hgqk', grouped, keys, precision=HIGHEST))
    places = jnp.arange(SEQ, dtype=jnp.int32)
    allowed = (places[None, :] <= places[:, None]) & (segment_ids[None, :] == segment_ids[:, None])
    scores = jnp.where(allowed, scores, NEG_FILL)
    peak = lax.optimization_barrier(jnp.max(scores, -1, keepdims=True))
    weights_exp = jnp.exp(scores - peak)
    probs = low(weights_exp / lax.optimization_barrier(jnp.sum(weights_exp, -1, keepdims=True)))
    mixed = jnp.einsum('hgqk,khd->qhgd', probs, values, precision=HIGHEST)
    return mixed.reshape(SEQ, HEADS * HEAD)

def run_layer(state, layer_params, cosine, sine_part, segments):
    query_weight, key_weight, value_weight, out_weight, gate_weight, up_weight, down_weight, mixer_gain, ffn_gain = layer_params
    inv_rms = lax.rsqrt(lax.optimization_barrier(jnp.mean(state * state, -1, keepdims=True)) + EPSILON)
    normed = low(state * inv_rms * mixer_gain)
    query_raw = low(low_back(matmul_high(normed, query_weight)))
    key_raw = low(low_back(matmul_high(normed, key_weight)))
    value_raw = low(low_back(matmul_high(normed, value_weight)))
    queries = low(rotate(query_raw.reshape(TOKENS, HEADS, HEAD), cosine, sine_part) * HEAD ** (-0.5))
    keys = low(rotate(key_raw.reshape(TOKENS, KV_HEADS, HEAD), cosine, sine_part))
    values = value_raw.reshape(TOKENS, KV_HEADS, HEAD)
    mixed = lax.map(jax.checkpoint(attend_sequence), (queries.reshape(NSEQ, SEQ, HEADS, HEAD), keys.reshape(NSEQ, SEQ, KV_HEADS, HEAD), values.reshape(NSEQ, SEQ, KV_HEADS, HEAD), segments))
    mixed = low(low_back(mixed.reshape(TOKENS, HEADS * HEAD)))
    hidden_state = state + low_back(matmul_high(mixed, out_weight))
    inv_rms_ffn = lax.rsqrt(lax.optimization_barrier(jnp.mean(hidden_state * hidden_state, -1, keepdims=True)) + EPSILON)
    ffn_normed = low(hidden_state * inv_rms_ffn * ffn_gain)
    gate_val = low_back(matmul_high(ffn_normed, gate_weight))
    up_val = low_back(matmul_high(ffn_normed, up_weight))
    activated = low(gate_val * jax.nn.sigmoid(gate_val) * up_val)
    return hidden_state + low_back(matmul_high(activated, down_weight.T))

def reference(tokens, query_weight, key_weight, value_weight, out_weight, gate_weight, up_weight, down_weight, attention_gain, feedforward_gain, positions, segments, cotangent):
    cosine, sine_part = rope_tables(positions.reshape(TOKENS))
    params = tuple((item.astype(jnp.float32) for item in (query_weight, key_weight, value_weight, out_weight, gate_weight, up_weight, down_weight, attention_gain, feedforward_gain)))

    def forward(features_first, weights):
        state = features_first.T
        for layer_idx in range(LAYERS):
            state = run_layer(state, tuple((item[layer_idx] for item in weights)), cosine, sine_part, segments)
        return state.T
    layer_out, pull_back = jax.vjp(forward, tokens.astype(jnp.float32), params)
    input_grad, param_grads = pull_back(cotangent.astype(jnp.float32))
    return (layer_out, input_grad, param_grads[0], param_grads[1], param_grads[2], param_grads[3], param_grads[4], param_grads[5], param_grads[6], param_grads[7], param_grads[8])
```

```python
import jax
import jax.numpy as jnp
from jax import lax
from jax.sharding import PartitionSpec as P

HEADS = 15
KV_HEADS = 5
HEAD = 64
SEQ = 1024
GROUPS = HEADS // KV_HEADS
EPSILON = 1e-05
NEG_FILL = -1e30
ROPE_BASE = 100000.0
LOW = jnp.bfloat16


def contract(left, right, left_dim, right_dim):
    return lax.dot_general(
        left, right, (((left_dim,), (right_dim,)), ((), ())), preferred_element_type=jnp.float32
    )


def rope_tables(positions):
    half_dim = HEAD // 2
    frequency = ROPE_BASE ** (-2.0 * jnp.arange(half_dim, dtype=jnp.float32) / HEAD)
    angle = positions.astype(jnp.float32)[:, None] * frequency[None, :]
    return jnp.cos(angle)[:, None, :], jnp.sin(angle)[:, None, :]


def rotate(values, cosine, sine):
    rows, width = values.shape
    split = values.reshape(rows, width // HEAD, HEAD)
    lower, upper = split[..., : HEAD // 2], split[..., HEAD // 2 :]
    turned = jnp.concatenate([lower * cosine - upper * sine, upper * cosine + lower * sine], -1)
    return turned.reshape(rows, width)


def swap_rows(value, step):
    count = lax.axis_size("rows")
    return lax.ppermute(value, "rows", [(i, i ^ step) for i in range(count)])


def rows_gather(block):
    count = lax.axis_size("rows")
    blocks = {0: block}
    step = count // 2
    while step:
        held = sorted(blocks)
        got = swap_rows(jnp.concatenate([blocks[i] for i in held], 0), step)
        for n, i in enumerate(held):
            blocks[i ^ step] = got[n * block.shape[0] : (n + 1) * block.shape[0]]
        step //= 2
    return jnp.concatenate([blocks[i] for i in range(count)], 0)


def rows_scatter(partial):
    count = lax.axis_size("rows")
    size = partial.shape[0] // count
    blocks = {i: partial[i * size : (i + 1) * size] for i in range(count)}
    step = 1
    while step < count:
        kept = [i for i in sorted(blocks) if not i & step]
        sent = jnp.concatenate([blocks[i ^ step] for i in kept], 0).astype(LOW)
        got = swap_rows(sent, step)
        blocks = {
            i: blocks[i] + got[n * size : (n + 1) * size].astype(jnp.float32)
            for n, i in enumerate(kept)
        }
        step *= 2
    return blocks[0]


def rows_exchange(chunks, row_index):
    count = lax.axis_size("rows")
    own = lax.dynamic_index_in_dim(chunks, row_index, 0)
    result = lax.dynamic_update_slice_in_dim(jnp.zeros_like(chunks), own, row_index, 0)
    for step in range(1, count):
        peer = row_index ^ step
        got = swap_rows(lax.dynamic_index_in_dim(chunks, peer, 0), step)
        result = lax.dynamic_update_slice_in_dim(result, got, peer, 0)
    return result


def dp_total(value):
    if lax.axis_size("dp") == 2:
        other = lax.ppermute(value, "dp", [(0, 1), (1, 0)])
        return value.astype(jnp.float32) + other.astype(jnp.float32)
    return lax.psum(value, "dp").astype(jnp.float32)


def spread(value, parts):
    return value.reshape(value.shape[0], parts, -1).transpose(1, 0, 2)


def unspread(value):
    return value.transpose(1, 0, 2).reshape(value.shape[1], -1)


def norm_forward(residual, gain):
    inv_rms = lax.rsqrt(jnp.mean(residual * residual, 1, keepdims=True) + EPSILON)
    return (residual * inv_rms * gain[None, :]).astype(LOW), inv_rms


def norm_backward(grad_normed, residual, inv_rms, gain):
    weighted = grad_normed * gain[None, :]
    summed = jnp.mean(weighted * residual, 1, keepdims=True)
    grad_residual = weighted * inv_rms - residual * (inv_rms**3 * summed)
    return grad_residual, jnp.sum(grad_normed * residual * inv_rms, 0)


def split_queries(values):
    return values.reshape(-1, KV_HEADS, GROUPS, HEAD).transpose(1, 2, 0, 3)


def split_keys(values):
    return values.reshape(-1, KV_HEADS, HEAD).transpose(1, 0, 2)


def attend_forward(queries, keys, values, allowed):

    def one_group(items):
        query_set, key_set, value_set = items
        scores = jnp.einsum("gqd,kd->gqk", query_set, key_set, preferred_element_type=jnp.float32)
        scores = jnp.where(allowed[None], scores, NEG_FILL)
        peak = jnp.max(scores, -1, keepdims=True)
        weights_exp = jnp.exp(scores - peak)
        denominator = jnp.sum(weights_exp, -1, keepdims=True)
        probs = (weights_exp / denominator).astype(LOW)
        mixed = jnp.einsum("gqk,kd->gqd", probs, value_set, preferred_element_type=jnp.float32)
        return mixed, peak[..., 0] + jnp.log(denominator[..., 0])

    mixed, log_norm = lax.map(
        one_group, (split_queries(queries), split_keys(keys), split_keys(values))
    )
    return mixed.transpose(2, 0, 1, 3).reshape(-1, HEADS * HEAD).astype(LOW), log_norm


def attend_backward(queries, keys, values, log_norm, grad_mixed, allowed):

    def one_group(items):
        query_set, key_set, value_set, log_set, grad_set = items
        scores = jnp.einsum("gqd,kd->gqk", query_set, key_set, preferred_element_type=jnp.float32)
        scores = jnp.where(allowed[None], scores, NEG_FILL)
        probs = jnp.exp(scores - log_set[..., None])
        grad_probs = jnp.einsum(
            "gqd,kd->gqk", grad_set, value_set, preferred_element_type=jnp.float32
        )
        inner = jnp.sum(probs * grad_probs, -1, keepdims=True)
        grad_scores = (probs * (grad_probs - inner)).astype(LOW)
        grad_query = jnp.einsum(
            "gqk,kd->gqd", grad_scores, key_set, preferred_element_type=jnp.float32
        )
        grad_key = jnp.einsum(
            "gqk,gqd->kd", grad_scores, query_set, preferred_element_type=jnp.float32
        )
        grad_value = jnp.einsum(
            "gqk,gqd->kd", probs.astype(LOW), grad_set, preferred_element_type=jnp.float32
        )
        return grad_query, grad_key, grad_value

    grad_query, grad_key, grad_value = lax.map(
        one_group,
        (
            split_queries(queries),
            split_keys(keys),
            split_keys(values),
            log_norm,
            split_queries(grad_mixed),
        ),
    )
    return (
        grad_query.transpose(2, 0, 1, 3).reshape(-1, HEADS * HEAD),
        grad_key.transpose(1, 0, 2).reshape(-1, KV_HEADS * HEAD),
        grad_value.transpose(1, 0, 2).reshape(-1, KV_HEADS * HEAD),
    )


def on_device(
    tokens,
    query_weight,
    key_weight,
    value_weight,
    out_weight,
    gate_weight,
    up_weight,
    down_weight,
    attention_gain,
    feedforward_gain,
    positions,
    segments,
    cotangent,
):
    row_index = lax.axis_index("rows")
    col_index = lax.axis_index("cols")
    row_count = lax.axis_size("rows")
    col_count = lax.axis_size("cols")
    feat_width, col_tokens = tokens.shape
    block_tokens = col_tokens // row_count
    half_block = block_tokens // 2
    layer_total = query_weight.shape[0]
    query_width = query_weight.shape[2]
    kv_width = key_weight.shape[2]
    all_queries = query_width * col_count
    all_kv = kv_width * col_count
    head_scale = HEAD ** (-0.5)

    deal = []
    for j in range(row_count):
        deal += [j, 2 * row_count - 1 - j]
    undeal = [deal.index(b) for b in range(2 * row_count)]

    def reorder(values, order):
        parts = [values[..., b * half_block : (b + 1) * half_block] for b in order]
        return jnp.concatenate(parts, -1)

    def to_token_blocks(values):
        chunks = spread(reorder(values, deal), row_count)
        return rows_exchange(chunks, row_index).reshape(-1, block_tokens).T

    def to_feature_blocks(values):
        chunks = values.astype(LOW).T.reshape(row_count, feat_width, block_tokens)
        return reorder(unspread(rows_exchange(chunks, row_index)), undeal).astype(jnp.float32)

    def blocks_here(values):
        dealt = reorder(values, deal).reshape(row_count, block_tokens)
        picked = [
            lax.dynamic_index_in_dim(dealt, row_index ^ i, 0, keepdims=False)
            for i in range(row_count)
        ]
        return jnp.concatenate(picked)

    places = blocks_here(jnp.arange(col_tokens, dtype=jnp.int32))
    own_positions = blocks_here(
        lax.dynamic_index_in_dim(positions, col_index, 0, keepdims=False)
    )[:block_tokens]
    doc = blocks_here(lax.dynamic_index_in_dim(segments, col_index, 0, keepdims=False))
    allowed = (places[None, :] <= places[:block_tokens, None]) & (
        doc[None, :] == doc[:block_tokens, None]
    )
    cosine, sine = rope_tables(own_positions)

    def attention_weights(layer):
        joint = jnp.concatenate([query_weight[layer], key_weight[layer], value_weight[layer]], 1)
        wide = lax.all_gather(joint, "cols", axis=0)
        wide = jnp.concatenate(
            [
                unspread(wide[:, :, :query_width]),
                unspread(wide[:, :, query_width : query_width + kv_width]),
                unspread(wide[:, :, query_width + kv_width :]),
            ],
            1,
        )
        joint_full = lax.all_gather(wide, "rows", axis=0, tiled=True)
        out_wide = unspread(lax.all_gather(out_weight[layer].T, "cols", axis=0))
        out_full = lax.all_gather(out_wide, "rows", axis=0, tiled=True)
        return joint_full, out_full

    def ffn_weights(layer):
        stacked = jnp.stack([gate_weight[layer], up_weight[layer], down_weight[layer]])
        hidden = stacked.shape[2]
        chunks = stacked.transpose(0, 2, 1).reshape(3, row_count, hidden // row_count, feat_width)
        whole = rows_exchange(chunks.transpose(1, 0, 2, 3), row_index)
        whole = whole.transpose(1, 2, 0, 3).reshape(3, hidden // row_count, -1)
        return [lax.all_gather(whole[i], "cols", axis=0, tiled=True) for i in range(3)]

    def attention_grads(joint_grad, out_grad):
        part = lax.psum_scatter(joint_grad.astype(LOW), "rows", scatter_dimension=0, tiled=True)
        part = jnp.concatenate(
            [
                spread(part[:, :all_queries], col_count),
                spread(part[:, all_queries : all_queries + all_kv], col_count),
                spread(part[:, all_queries + all_kv :], col_count),
            ],
            2,
        )
        joint = dp_total(lax.psum_scatter(part, "cols", scatter_dimension=0))
        out = lax.psum_scatter(out_grad.astype(LOW), "rows", scatter_dimension=0, tiled=True)
        out = dp_total(lax.psum_scatter(spread(out, col_count), "cols", scatter_dimension=0)).T
        return (
            joint[:, :query_width],
            joint[:, query_width : query_width + kv_width],
            joint[:, query_width + kv_width :],
            out,
        )

    def ffn_grads(grads):
        parts = jnp.stack(
            [
                lax.psum_scatter(g.astype(LOW), "cols", scatter_dimension=0, tiled=True)
                for g in grads
            ]
        )
        hidden_part = parts.shape[1]
        chunks = parts.reshape(3, hidden_part, row_count, feat_width).transpose(2, 0, 1, 3)
        mine = rows_exchange(chunks, row_index).transpose(1, 3, 0, 2)
        return dp_total(mine.reshape(3, feat_width, row_count * hidden_part))

    attention_ws = [attention_weights(n) for n in range(layer_total)]
    ffn_ws = [ffn_weights(n) for n in range(layer_total)]

    residual = to_token_blocks(tokens).astype(jnp.float32)
    saved = []
    for layer in range(layer_total):
        joint_full, out_full = attention_ws[layer]
        gate_full, up_full, down_full = ffn_ws[layer]
        normed, mixer_scale = norm_forward(residual, attention_gain[layer])
        projected = contract(normed, joint_full, 1, 0).astype(LOW).astype(jnp.float32)
        queries = (rotate(projected[:, :all_queries], cosine, sine) * head_scale).astype(LOW)
        own_kv = jnp.concatenate(
            [
                rotate(projected[:, all_queries : all_queries + all_kv], cosine, sine),
                projected[:, all_queries + all_kv :],
            ],
            1,
        ).astype(LOW)
        both = rows_gather(own_kv)
        keys, values = both[:, :all_kv], both[:, all_kv:]
        mixed, log_norm = attend_forward(queries, keys, values, allowed)
        hidden = residual + contract(mixed, out_full, 1, 1)
        ffn_normed, ffn_scale = norm_forward(hidden, feedforward_gain[layer])
        ffn_all = rows_gather(ffn_normed)
        gate = contract(ffn_all, gate_full, 1, 1)
        up = contract(ffn_all, up_full, 1, 1)
        activated = (gate * jax.nn.sigmoid(gate) * up).astype(LOW)
        ffn_out = rows_scatter(contract(activated, down_full, 1, 0))
        saved.append(
            (residual, mixer_scale, normed, queries, keys, values, log_norm, mixed, hidden)
            + (ffn_scale, ffn_all, gate, up, activated)
        )
        residual = hidden + ffn_out

    weight_grads = [None] * layer_total
    gain_grads = [None] * layer_total
    grad = to_token_blocks(cotangent).astype(jnp.float32)
    for layer in reversed(range(layer_total)):
        joint_full, out_full = attention_ws[layer]
        gate_full, up_full, down_full = ffn_ws[layer]
        (layer_input, mixer_scale, normed, queries, keys, values, log_norm, mixed, hidden) = saved[
            layer
        ][:9]
        ffn_scale, ffn_all, gate, up, activated = saved[layer][9:]
        grad_all = rows_gather(grad.astype(LOW))
        grad_act = contract(grad_all, down_full, 1, 1)
        down_grad = contract(activated, grad_all, 0, 0)
        sig = jax.nn.sigmoid(gate)
        grad_gate = (grad_act * up * sig * (1.0 + gate * (1.0 - sig))).astype(LOW)
        grad_up = (grad_act * gate * sig).astype(LOW)
        grad_ffn_normed = rows_scatter(
            contract(grad_gate, gate_full, 1, 0) + contract(grad_up, up_full, 1, 0)
        )
        gate_grad = contract(grad_gate, ffn_all, 0, 0)
        up_grad = contract(grad_up, ffn_all, 0, 0)
        ffn_norm_grad, ffn_gain_grad = norm_backward(
            grad_ffn_normed, hidden, ffn_scale, feedforward_gain[layer]
        )
        grad_hidden = grad + ffn_norm_grad
        grad_low = grad_hidden.astype(LOW)
        grad_mixed = contract(grad_low, out_full, 1, 0).astype(LOW)
        out_grad = contract(grad_low, mixed, 0, 0)
        grad_query, grad_key, grad_value = attend_backward(
            queries, keys, values, log_norm, grad_mixed, allowed
        )
        grad_kv = rows_scatter(jnp.concatenate([grad_key, grad_value], 1))
        grad_joint = jnp.concatenate(
            [
                rotate(grad_query, cosine, -sine) * head_scale,
                rotate(grad_kv[:, :all_kv], cosine, -sine),
                grad_kv[:, all_kv:],
            ],
            1,
        ).astype(LOW)
        grad_normed = contract(grad_joint, joint_full, 1, 1)
        joint_grad = contract(normed, grad_joint, 0, 0)
        mixer_norm_grad, mixer_gain_grad = norm_backward(
            grad_normed, layer_input, mixer_scale, attention_gain[layer]
        )
        grad = grad_hidden + mixer_norm_grad
        ffn_parts = ffn_grads([gate_grad, up_grad, down_grad])
        weight_grads[layer] = attention_grads(joint_grad, out_grad) + (
            ffn_parts[0],
            ffn_parts[1],
            ffn_parts[2],
        )
        gain_grads[layer] = jnp.stack([mixer_gain_grad, ffn_gain_grad])

    gain_total = lax.psum(jnp.stack(gain_grads), ("dp", "rows", "cols"))
    totals = [jnp.stack([weight_grads[n][i] for n in range(layer_total)]) for i in range(7)]
    return (
        to_feature_blocks(residual),
        to_feature_blocks(grad),
        totals[0],
        totals[1],
        totals[2],
        totals[3],
        totals[4],
        totals[5],
        totals[6],
        gain_total[:, 0],
        gain_total[:, 1],
    )


def solution(mesh):
    whole = P("rows", ("dp", "cols"))
    weight = P(None, "rows", "cols")
    flipped = P(None, "cols", "rows")
    return jax.shard_map(
        on_device,
        mesh=mesh,
        in_specs=(whole, weight, weight, weight, flipped, weight, weight, weight)
        + (P(), P(), P("dp", None), P("dp", None), whole),
        out_specs=(whole, whole, weight, weight, weight, flipped, weight, weight, weight, P(), P()),
        check_vma=False,
    )
```

```python
import jax
import jax.numpy as jnp
from jax import lax
from jax.experimental import pallas as pl
from jax.sharding import PartitionSpec as P

HEADS = 15
KV_HEADS = 5
HEAD = 64
SEQ = 1024
GROUPS = HEADS // KV_HEADS
EPSILON = 1e-05
NEG_FILL = -1e30
ROPE_BASE = 100000.0
LOW = jnp.bfloat16


def contract(left, right, left_dim, right_dim):
    return lax.dot_general(
        left, right, (((left_dim,), (right_dim,)), ((), ())), preferred_element_type=jnp.float32
    )


def rope_tables(positions):
    half_dim = HEAD // 2
    frequency = ROPE_BASE ** (-2.0 * jnp.arange(half_dim, dtype=jnp.float32) / HEAD)
    angle = frequency[:, None] * positions.astype(jnp.float32)[None, :]
    return jnp.cos(angle), jnp.sin(angle)


def swap_rows(value, step):
    count = lax.axis_size("rows")
    return lax.ppermute(value, "rows", [(i, i ^ step) for i in range(count)])


def rows_gather(block):
    count = lax.axis_size("rows")
    blocks = {0: block}
    step = count // 2
    while step:
        held = sorted(blocks)
        got = swap_rows(jnp.concatenate([blocks[i] for i in held], 0), step)
        for n, i in enumerate(held):
            blocks[i ^ step] = got[n * block.shape[0] : (n + 1) * block.shape[0]]
        step //= 2
    return jnp.concatenate([blocks[i] for i in range(count)], 0)


def rows_scatter(partial):
    count = lax.axis_size("rows")
    size = partial.shape[0] // count
    blocks = {i: partial[i * size : (i + 1) * size] for i in range(count)}
    step = 1
    while step < count:
        kept = [i for i in sorted(blocks) if not i & step]
        sent = jnp.concatenate([blocks[i ^ step] for i in kept], 0).astype(LOW)
        got = swap_rows(sent, step)
        blocks = {
            i: blocks[i] + got[n * size : (n + 1) * size].astype(jnp.float32)
            for n, i in enumerate(kept)
        }
        step *= 2
    return blocks[0]


def rows_exchange(chunks, row_index):
    count = lax.axis_size("rows")
    own = lax.dynamic_index_in_dim(chunks, row_index, 0)
    result = lax.dynamic_update_slice_in_dim(jnp.zeros_like(chunks), own, row_index, 0)
    for step in range(1, count):
        peer = row_index ^ step
        got = swap_rows(lax.dynamic_index_in_dim(chunks, peer, 0), step)
        result = lax.dynamic_update_slice_in_dim(result, got, peer, 0)
    return result


def swap_dp(value, step):
    count = lax.axis_size("dp")
    return lax.ppermute(value, "dp", [(i, i ^ step) for i in range(count)])


def spread(value, parts):
    return value.reshape(value.shape[0], parts, -1).transpose(1, 0, 2)


def unspread(value):
    return value.transpose(1, 0, 2).reshape(value.shape[1], -1)


def norm_forward(residual, gain):
    inv_rms = lax.rsqrt(jnp.mean(residual * residual, 1, keepdims=True) + EPSILON)
    return (residual * inv_rms * gain[None, :]).astype(LOW), inv_rms


def norm_backward(grad_normed, residual, inv_rms, gain):
    weighted = grad_normed * gain[None, :]
    summed = jnp.mean(weighted * residual, 1, keepdims=True)
    grad_residual = weighted * inv_rms - residual * (inv_rms**3 * summed)
    return grad_residual, jnp.sum(grad_normed * residual * inv_rms, 0)


def turn(values, cosine, sine):
    width, count = values.shape
    split = values.reshape(width // HEAD, 2, HEAD // 2, count)
    lower, upper = split[:, 0], split[:, 1]
    turned = jnp.stack([lower * cosine - upper * sine, upper * cosine + lower * sine], 1)
    return turned.reshape(width, count)


def forward_kernel(query_ref, key_ref, value_ref, bias_ref, mixed_ref, log_ref):
    parts, _, size = key_ref.shape
    for i in range(GROUPS):
        rows = pl.ds(i * HEAD, HEAD)
        query = query_ref[rows, :]
        scores = [
            contract(key_ref[j], query, 0, 0) + bias_ref[pl.ds(j * size, size), :]
            for j in range(parts)
        ]
        peak = jnp.max(scores[0], 0, keepdims=True)
        for j in range(1, parts):
            peak = jnp.maximum(peak, jnp.max(scores[j], 0, keepdims=True))
        total = jnp.zeros_like(peak)
        mixed = jnp.zeros((HEAD, query.shape[1]), jnp.float32)
        for j in range(parts):
            weights = jnp.exp(scores[j] - peak)
            total = total + jnp.sum(weights, 0, keepdims=True)
            mixed = mixed + contract(value_ref[j], weights.astype(LOW), 1, 0)
        mixed_ref[rows, :] = (mixed / total).astype(LOW)
        log_ref[0, pl.ds(i, 1), :] = peak + jnp.log(total)


def backward_kernel(
    query_ref, key_ref, value_ref, bias_ref, mixed_ref, log_ref, grad_ref,
    grad_query_ref, grad_key_ref, grad_value_ref,
):
    parts, _, size = key_ref.shape
    for i in range(GROUPS):
        rows = pl.ds(i * HEAD, HEAD)
        query, grad = query_ref[rows, :], grad_ref[rows, :]
        wide = grad.astype(jnp.float32)
        inner = jnp.sum(wide * mixed_ref[rows, :].astype(jnp.float32), 0, keepdims=True)
        log_norm = log_ref[0, pl.ds(i, 1), :]
        grad_query = jnp.zeros((HEAD, query.shape[1]), jnp.float32)
        for j in range(parts):
            key, value = key_ref[j], value_ref[j]
            scores = contract(key, query, 0, 0) + bias_ref[pl.ds(j * size, size), :]
            probs = jnp.exp(scores - log_norm)
            grad_probs = contract(value, grad, 0, 0)
            grad_scores = (probs * (grad_probs - inner)).astype(LOW)
            grad_query = grad_query + contract(key, grad_scores, 1, 0)
            grad_key = contract(query, grad_scores, 1, 1)
            grad_value = contract(grad, probs.astype(LOW), 1, 1)
            if i == 0:
                grad_key_ref[j] = grad_key
                grad_value_ref[j] = grad_value
            else:
                grad_key_ref[j] += grad_key
                grad_value_ref[j] += grad_value
        grad_query_ref[rows, :] = grad_query


def attention_specs(queries, both):
    parts, _, size = both.shape
    count = queries.shape[1]
    per_query = pl.BlockSpec((GROUPS * HEAD, count), lambda g: (g, 0))
    key = pl.BlockSpec((parts, HEAD, size), lambda g: (0, g, 0))
    value = pl.BlockSpec((parts, HEAD, size), lambda g: (0, g + KV_HEADS, 0))
    bias = pl.BlockSpec((parts * size, count), lambda g: (0, 0))
    log = pl.BlockSpec((1, 8, count), lambda g: (g, 0, 0))
    work = HEADS * count * parts * size
    return per_query, key, value, bias, log, work


def attend_forward(queries, both, bias):
    per_query, key, value, shared, log, work = attention_specs(queries, both)
    return pl.pallas_call(
        forward_kernel,
        grid=(KV_HEADS,),
        in_specs=[per_query, key, value, shared],
        out_specs=[per_query, log],
        out_shape=[
            jax.ShapeDtypeStruct(queries.shape, LOW),
            jax.ShapeDtypeStruct((KV_HEADS, 8, queries.shape[1]), jnp.float32),
        ],
        cost_estimate=pl.CostEstimate(
            flops=4 * HEAD * work, transcendentals=work, bytes_accessed=4 << 20
        ),
        name="attend_forward",
    )(queries, both, both, bias)


def attend_backward(queries, both, bias, mixed, log_norm, grad_mixed):
    per_query, key, value, shared, log, work = attention_specs(queries, both)
    parts, _, size = both.shape
    grad_kv = jax.ShapeDtypeStruct((parts, KV_HEADS * HEAD, size), jnp.float32)
    return pl.pallas_call(
        backward_kernel,
        grid=(KV_HEADS,),
        in_specs=[per_query, key, value, shared, per_query, log, per_query],
        out_specs=[per_query, key, key],
        out_shape=[jax.ShapeDtypeStruct(queries.shape, jnp.float32), grad_kv, grad_kv],
        cost_estimate=pl.CostEstimate(
            flops=10 * HEAD * work, transcendentals=work, bytes_accessed=8 << 20
        ),
        name="attend_backward",
    )(queries, both, both, bias, mixed, log_norm, grad_mixed)


def on_device(
    tokens,
    query_weight,
    key_weight,
    value_weight,
    out_weight,
    gate_weight,
    up_weight,
    down_weight,
    attention_gain,
    feedforward_gain,
    positions,
    segments,
    cotangent,
):
    row_index = lax.axis_index("rows")
    col_index = lax.axis_index("cols")
    dp_index = lax.axis_index("dp")
    dp_count = lax.axis_size("dp")
    row_count = lax.axis_size("rows")
    col_count = lax.axis_size("cols")
    feat_width, col_tokens = tokens.shape
    block_tokens = col_tokens // row_count
    half_block = block_tokens // 2
    layer_total = query_weight.shape[0]
    query_width = query_weight.shape[2]
    kv_width = key_weight.shape[2]
    all_queries = query_width * col_count
    all_kv = kv_width * col_count
    head_scale = HEAD ** (-0.5)

    deal = []
    for j in range(row_count):
        deal += [j, 2 * row_count - 1 - j]
    undeal = [deal.index(b) for b in range(2 * row_count)]

    def reorder(values, order):
        parts = [values[..., b * half_block : (b + 1) * half_block] for b in order]
        return jnp.concatenate(parts, -1)

    def to_token_blocks(values):
        chunks = spread(reorder(values, deal), row_count)
        return rows_exchange(chunks, row_index).reshape(-1, block_tokens).T

    def to_feature_blocks(values):
        chunks = values.astype(LOW).T.reshape(row_count, feat_width, block_tokens)
        return reorder(unspread(rows_exchange(chunks, row_index)), undeal).astype(jnp.float32)

    def blocks_here(values):
        dealt = reorder(values, deal).reshape(row_count, block_tokens)
        picked = [
            lax.dynamic_index_in_dim(dealt, row_index ^ i, 0, keepdims=False)
            for i in range(row_count)
        ]
        return jnp.concatenate(picked)

    places = blocks_here(jnp.arange(col_tokens, dtype=jnp.int32))
    own_positions = blocks_here(
        lax.dynamic_index_in_dim(positions, col_index, 0, keepdims=False)
    )[:block_tokens]
    doc = blocks_here(lax.dynamic_index_in_dim(segments, col_index, 0, keepdims=False))
    allowed = (places[:, None] <= places[None, :block_tokens]) & (
        doc[:, None] == doc[None, :block_tokens]
    )
    bias = jnp.where(allowed, 0.0, NEG_FILL)
    cosine, sine = rope_tables(own_positions)

    def attention_weights(layer):
        joint = jnp.concatenate(
            [query_weight[layer], key_weight[layer], value_weight[layer], out_weight[layer].T], 1
        )
        wide = lax.all_gather(joint, "cols", axis=0, tiled=True)
        wide = wide.reshape(col_count, feat_width, -1)
        ends = [query_width, query_width + kv_width, query_width + 2 * kv_width]
        parts = [unspread(part) for part in jnp.split(wide, ends, 2)]
        joint_full = lax.all_gather(
            jnp.concatenate(parts[:3], 1), "rows", axis=0, tiled=True
        )
        out_full = lax.all_gather(parts[3], "rows", axis=0, tiled=True)
        return joint_full, out_full

    def ffn_weights(layer):
        stacked = jnp.stack([gate_weight[layer], up_weight[layer], down_weight[layer]])
        chunks = stacked.transpose(0, 2, 1).reshape(3, row_count, 2, -1, feat_width)
        half = lax.dynamic_index_in_dim(chunks, dp_index % 2, 2, keepdims=False)
        whole = rows_exchange(half.transpose(1, 0, 2, 3), row_index)
        whole = whole.transpose(1, 2, 0, 3).reshape(-1, row_count * feat_width)
        own = lax.all_gather(whole, "cols", axis=0, tiled=True)
        other = swap_dp(own, 1)
        own = own.reshape(col_count, 3, -1, row_count * feat_width)
        other = other.reshape(own.shape)
        return [
            jnp.concatenate([own[:, i], other[:, i]], 0).reshape(-1, row_count * feat_width)
            for i in range(3)
        ]

    def attention_grads(joint_grad, out_grad):
        part = lax.psum_scatter(joint_grad.astype(LOW), "rows", scatter_dimension=0, tiled=True)
        out = lax.psum_scatter(out_grad.astype(LOW), "rows", scatter_dimension=0, tiled=True)
        ends = [all_queries, all_queries + all_kv]
        parts = [spread(p, col_count) for p in jnp.split(part, ends, 1) + [out]]
        joint = jnp.concatenate(parts, 2)
        joint = joint.reshape(col_count * feat_width, -1)
        joint = lax.psum_scatter(joint, "cols", scatter_dimension=0, tiled=True)
        step = 1
        while step < dp_count:
            joint = joint.astype(jnp.float32) + swap_dp(joint.astype(LOW), step).astype(jnp.float32)
            step *= 2
        ends = [query_width, query_width + kv_width, query_width + 2 * kv_width]
        parts = jnp.split(joint, ends, 1)
        return parts[0], parts[1], parts[2], parts[3].T

    def ffn_grads(grads):
        stacked = jnp.stack([g.astype(LOW).reshape(2, col_count, -1, g.shape[1]) for g in grads], 2)
        half = stacked[0].astype(jnp.float32) + swap_dp(stacked[1], 1).astype(jnp.float32)
        half = half.astype(LOW).reshape(-1, half.shape[-1])
        mine = lax.psum_scatter(half, "cols", scatter_dimension=0, tiled=True)
        step = 2
        while step < dp_count:
            mine = (mine.astype(jnp.float32) + swap_dp(mine, step).astype(jnp.float32)).astype(LOW)
            step *= 2
        chunks = mine.reshape(3, -1, row_count, feat_width).transpose(2, 0, 1, 3)
        mine = rows_exchange(chunks, row_index)
        other = swap_dp(mine, 1)
        first = dp_index % 2 == 0
        both = jnp.stack([jnp.where(first, mine, other), jnp.where(first, other, mine)], 2)
        both = both.transpose(1, 4, 0, 2, 3)
        return both.reshape(3, feat_width, -1).astype(jnp.float32)

    def everywhere(value):
        for axis in ("rows", "dp", "cols"):
            count = lax.axis_size(axis)
            step = 1
            while step < count:
                value = value + lax.ppermute(value, axis, [(i, i ^ step) for i in range(count)])
                step *= 2
        return value

    attention_ws = [attention_weights(n) for n in range(layer_total)]
    ffn_ws = [ffn_weights(n) for n in range(layer_total)]

    residual = to_token_blocks(tokens).astype(jnp.float32)
    saved = []
    for layer in range(layer_total):
        joint_full, out_full = attention_ws[layer]
        gate_full, up_full, down_full = ffn_ws[layer]
        normed, mixer_scale = norm_forward(residual, attention_gain[layer])
        projected = contract(joint_full, normed, 0, 1).astype(LOW).astype(jnp.float32)
        queries = (turn(projected[:all_queries], cosine, sine) * head_scale).astype(LOW)
        own_kv = jnp.concatenate(
            [
                turn(projected[all_queries : all_queries + all_kv], cosine, sine),
                projected[all_queries + all_kv :],
            ],
            0,
        ).astype(LOW)
        both = rows_gather(own_kv).reshape(row_count, 2 * all_kv, block_tokens)
        mixed, log_norm = attend_forward(queries, both, bias)
        hidden = residual + contract(mixed, out_full, 0, 1)
        ffn_normed, ffn_scale = norm_forward(hidden, feedforward_gain[layer])
        ffn_all = rows_gather(ffn_normed)
        gate = contract(ffn_all, gate_full, 1, 1)
        up = contract(ffn_all, up_full, 1, 1)
        activated = (gate * jax.nn.sigmoid(gate) * up).astype(LOW)
        ffn_out = rows_scatter(contract(activated, down_full, 1, 0))
        saved.append(
            (residual, mixer_scale, normed, queries, both, log_norm, mixed, hidden)
            + (ffn_scale, ffn_all, gate, up, activated)
        )
        residual = hidden + ffn_out

    weight_grads = [None] * layer_total
    gain_grads = [None] * layer_total
    grad = to_token_blocks(cotangent).astype(jnp.float32)
    for layer in reversed(range(layer_total)):
        joint_full, out_full = attention_ws[layer]
        gate_full, up_full, down_full = ffn_ws[layer]
        layer_input, mixer_scale, normed, queries, both, log_norm, mixed, hidden = saved[layer][:8]
        ffn_scale, ffn_all, gate, up, activated = saved[layer][8:]
        grad_all = rows_gather(grad.astype(LOW))
        grad_act = contract(grad_all, down_full, 1, 1)
        down_grad = contract(activated, grad_all, 0, 0)
        sig = jax.nn.sigmoid(gate)
        grad_gate = (grad_act * up * sig * (1.0 + gate * (1.0 - sig))).astype(LOW)
        grad_up = (grad_act * gate * sig).astype(LOW)
        grad_ffn_normed = rows_scatter(
            contract(grad_gate, gate_full, 1, 0) + contract(grad_up, up_full, 1, 0)
        )
        gate_grad = contract(grad_gate, ffn_all, 0, 0)
        up_grad = contract(grad_up, ffn_all, 0, 0)
        ffn_norm_grad, ffn_gain_grad = norm_backward(
            grad_ffn_normed, hidden, ffn_scale, feedforward_gain[layer]
        )
        grad_hidden = grad + ffn_norm_grad
        grad_low = grad_hidden.astype(LOW)
        grad_mixed = contract(out_full, grad_low, 0, 1).astype(LOW)
        out_grad = contract(grad_low, mixed, 0, 1)
        grad_query, grad_key, grad_value = attend_backward(
            queries, both, bias, mixed, log_norm, grad_mixed
        )
        grad_kv = jnp.concatenate([grad_key, grad_value], 1).reshape(-1, block_tokens)
        grad_kv = rows_scatter(grad_kv)
        grad_joint = jnp.concatenate(
            [
                turn(grad_query, cosine, -sine) * head_scale,
                turn(grad_kv[:all_kv], cosine, -sine),
                grad_kv[all_kv:],
            ],
            0,
        ).astype(LOW)
        grad_normed = contract(grad_joint, joint_full, 0, 1)
        joint_grad = contract(normed, grad_joint, 0, 1)
        mixer_norm_grad, mixer_gain_grad = norm_backward(
            grad_normed, layer_input, mixer_scale, attention_gain[layer]
        )
        grad = grad_hidden + mixer_norm_grad
        ffn_parts = ffn_grads([gate_grad, up_grad, down_grad])
        weight_grads[layer] = attention_grads(joint_grad, out_grad) + (
            ffn_parts[0],
            ffn_parts[1],
            ffn_parts[2],
        )
        gain_grads[layer] = jnp.stack([mixer_gain_grad, ffn_gain_grad])

    gain_total = everywhere(jnp.stack(gain_grads))
    totals = [jnp.stack([weight_grads[n][i] for n in range(layer_total)]) for i in range(7)]
    return (
        to_feature_blocks(residual),
        to_feature_blocks(grad),
        totals[0],
        totals[1],
        totals[2],
        totals[3],
        totals[4],
        totals[5],
        totals[6],
        gain_total[:, 0],
        gain_total[:, 1],
    )


def solution(mesh):
    whole = P("rows", ("dp", "cols"))
    weight = P(None, "rows", "cols")
    flipped = P(None, "cols", "rows")
    return jax.shard_map(
        on_device,
        mesh=mesh,
        in_specs=(whole, weight, weight, weight, flipped, weight, weight, weight)
        + (P(), P(), P("dp", None), P("dp", None), whole),
        out_specs=(whole, whole, weight, weight, weight, flipped, weight, weight, weight, P(), P()),
        check_vma=False,
    )
```

```python
import jax
import jax.numpy as jnp
from jax import lax
from jax.experimental import pallas as pl
from jax.sharding import PartitionSpec as P

HEADS = 15
KV_HEADS = 5
HEAD = 64
SEQ = 1024
GROUPS = HEADS // KV_HEADS
EPSILON = 1e-05
NEG_FILL = -1e30
ROPE_BASE = 100000.0
LOW = jnp.bfloat16


def contract(left, right, left_dim, right_dim):
    return lax.dot_general(
        left, right, (((left_dim,), (right_dim,)), ((), ())), preferred_element_type=jnp.float32
    )


def rope_tables(positions):
    half_dim = HEAD // 2
    frequency = ROPE_BASE ** (-2.0 * jnp.arange(half_dim, dtype=jnp.float32) / HEAD)
    angle = frequency[:, None] * positions.astype(jnp.float32)[None, :]
    return jnp.cos(angle), jnp.sin(angle)


def swap_rows(value, step):
    count = lax.axis_size("rows")
    return lax.ppermute(value, "rows", [(i, i ^ step) for i in range(count)])


def rows_gather(block):
    count = lax.axis_size("rows")
    blocks = {0: block}
    step = count // 2
    while step:
        held = sorted(blocks)
        got = swap_rows(jnp.concatenate([blocks[i] for i in held], 0), step)
        for n, i in enumerate(held):
            blocks[i ^ step] = got[n * block.shape[0] : (n + 1) * block.shape[0]]
        step //= 2
    return jnp.concatenate([blocks[i] for i in range(count)], 0)


def rows_scatter(partial):
    count = lax.axis_size("rows")
    size = partial.shape[0] // count
    blocks = {i: partial[i * size : (i + 1) * size] for i in range(count)}
    step = 1
    while step < count:
        kept = [i for i in sorted(blocks) if not i & step]
        sent = jnp.concatenate([blocks[i ^ step] for i in kept], 0).astype(LOW)
        got = swap_rows(sent, step)
        blocks = {
            i: blocks[i] + got[n * size : (n + 1) * size].astype(jnp.float32)
            for n, i in enumerate(kept)
        }
        step *= 2
    return blocks[0]


def rows_exchange(chunks, row_index):
    count = lax.axis_size("rows")
    own = lax.dynamic_index_in_dim(chunks, row_index, 0)
    result = lax.dynamic_update_slice_in_dim(jnp.zeros_like(chunks), own, row_index, 0)
    for step in range(1, count):
        peer = row_index ^ step
        got = swap_rows(lax.dynamic_index_in_dim(chunks, peer, 0), step)
        result = lax.dynamic_update_slice_in_dim(result, got, peer, 0)
    return result


def after(value, earlier):
    return lax.optimization_barrier((value, earlier))[0]


def relabel(blocks, row_index):
    count = lax.axis_size("rows")
    split = blocks.reshape(count, -1, blocks.shape[1])
    picked = [
        lax.dynamic_index_in_dim(split, row_index ^ i, 0, keepdims=False) for i in range(count)
    ]
    return jnp.concatenate(picked, 0)


def swap_dp(value, step):
    count = lax.axis_size("dp")
    return lax.ppermute(value, "dp", [(i, i ^ step) for i in range(count)])


def spread(value, parts):
    return value.reshape(value.shape[0], parts, -1).transpose(1, 0, 2)


def unspread(value):
    return value.transpose(1, 0, 2).reshape(value.shape[1], -1)


def norm_forward(residual, gain):
    inv_rms = lax.rsqrt(jnp.mean(residual * residual, 1, keepdims=True) + EPSILON)
    return (residual * inv_rms * gain[None, :]).astype(LOW), inv_rms


def norm_backward(grad_normed, residual, inv_rms, gain):
    weighted = grad_normed * gain[None, :]
    summed = jnp.mean(weighted * residual, 1, keepdims=True)
    grad_residual = weighted * inv_rms - residual * (inv_rms**3 * summed)
    return grad_residual, jnp.sum(grad_normed * residual * inv_rms, 0)


def turn(values, cosine, sine):
    width, count = values.shape
    split = values.reshape(width // HEAD, 2, HEAD // 2, count)
    lower, upper = split[:, 0], split[:, 1]
    turned = jnp.stack([lower * cosine - upper * sine, upper * cosine + lower * sine], 1)
    return turned.reshape(width, count)


def forward_kernel(query_ref, key_ref, value_ref, bias_ref, mixed_ref, log_ref):
    parts, _, size = key_ref.shape
    for i in range(GROUPS):
        rows = pl.ds(i * HEAD, HEAD)
        query = query_ref[rows, :]
        scores = [
            contract(key_ref[j], query, 0, 0) + bias_ref[pl.ds(j * size, size), :]
            for j in range(parts)
        ]
        peak = jnp.max(scores[0], 0, keepdims=True)
        for j in range(1, parts):
            peak = jnp.maximum(peak, jnp.max(scores[j], 0, keepdims=True))
        total = jnp.zeros_like(peak)
        mixed = jnp.zeros((HEAD, query.shape[1]), jnp.float32)
        for j in range(parts):
            weights = jnp.exp(scores[j] - peak)
            total = total + jnp.sum(weights, 0, keepdims=True)
            mixed = mixed + contract(value_ref[j], weights.astype(LOW), 1, 0)
        mixed_ref[rows, :] = (mixed / total).astype(LOW)
        log_ref[0, pl.ds(i, 1), :] = peak + jnp.log(total)


def backward_kernel(
    query_ref, key_ref, value_ref, bias_ref, mixed_ref, log_ref, grad_ref,
    grad_query_ref, grad_key_ref, grad_value_ref,
):
    parts, _, size = key_ref.shape
    for i in range(GROUPS):
        rows = pl.ds(i * HEAD, HEAD)
        query, grad = query_ref[rows, :], grad_ref[rows, :]
        wide = grad.astype(jnp.float32)
        inner = jnp.sum(wide * mixed_ref[rows, :].astype(jnp.float32), 0, keepdims=True)
        log_norm = log_ref[0, pl.ds(i, 1), :]
        grad_query = jnp.zeros((HEAD, query.shape[1]), jnp.float32)
        for j in range(parts):
            key, value = key_ref[j], value_ref[j]
            scores = contract(key, query, 0, 0) + bias_ref[pl.ds(j * size, size), :]
            probs = jnp.exp(scores - log_norm)
            grad_probs = contract(value, grad, 0, 0)
            grad_scores = (probs * (grad_probs - inner)).astype(LOW)
            grad_query = grad_query + contract(key, grad_scores, 1, 0)
            grad_key = contract(query, grad_scores, 1, 1)
            grad_value = contract(grad, probs.astype(LOW), 1, 1)
            if i == 0:
                grad_key_ref[j] = grad_key
                grad_value_ref[j] = grad_value
            else:
                grad_key_ref[j] += grad_key
                grad_value_ref[j] += grad_value
        grad_query_ref[rows, :] = grad_query


def attention_specs(queries, both):
    parts, _, size = both.shape
    count = queries.shape[1]
    per_query = pl.BlockSpec((GROUPS * HEAD, count), lambda g: (g, 0))
    key = pl.BlockSpec((parts, HEAD, size), lambda g: (0, g, 0))
    value = pl.BlockSpec((parts, HEAD, size), lambda g: (0, g + KV_HEADS, 0))
    bias = pl.BlockSpec((parts * size, count), lambda g: (0, 0))
    log = pl.BlockSpec((1, 8, count), lambda g: (g, 0, 0))
    work = HEADS * count * parts * size
    return per_query, key, value, bias, log, work


def attend_forward(queries, both, bias):
    per_query, key, value, shared, log, work = attention_specs(queries, both)
    return pl.pallas_call(
        forward_kernel,
        grid=(KV_HEADS,),
        in_specs=[per_query, key, value, shared],
        out_specs=[per_query, log],
        out_shape=[
            jax.ShapeDtypeStruct(queries.shape, LOW),
            jax.ShapeDtypeStruct((KV_HEADS, 8, queries.shape[1]), jnp.float32),
        ],
        cost_estimate=pl.CostEstimate(
            flops=4 * HEAD * work, transcendentals=work, bytes_accessed=4 << 20
        ),
        name="attend_forward",
    )(queries, both, both, bias)


def attend_backward(queries, both, bias, mixed, log_norm, grad_mixed):
    per_query, key, value, shared, log, work = attention_specs(queries, both)
    parts, _, size = both.shape
    grad_kv = jax.ShapeDtypeStruct((parts, KV_HEADS * HEAD, size), jnp.float32)
    return pl.pallas_call(
        backward_kernel,
        grid=(KV_HEADS,),
        in_specs=[per_query, key, value, shared, per_query, log, per_query],
        out_specs=[per_query, key, key],
        out_shape=[jax.ShapeDtypeStruct(queries.shape, jnp.float32), grad_kv, grad_kv],
        cost_estimate=pl.CostEstimate(
            flops=10 * HEAD * work, transcendentals=work, bytes_accessed=8 << 20
        ),
        name="attend_backward",
    )(queries, both, both, bias, mixed, log_norm, grad_mixed)


def on_device(
    tokens,
    query_weight,
    key_weight,
    value_weight,
    out_weight,
    gate_weight,
    up_weight,
    down_weight,
    attention_gain,
    feedforward_gain,
    positions,
    segments,
    cotangent,
):
    row_index = lax.axis_index("rows")
    col_index = lax.axis_index("cols")
    dp_index = lax.axis_index("dp")
    dp_count = lax.axis_size("dp")
    row_count = lax.axis_size("rows")
    col_count = lax.axis_size("cols")
    feat_width, col_tokens = tokens.shape
    block_tokens = col_tokens // row_count
    half_block = block_tokens // 2
    layer_total = query_weight.shape[0]
    query_width = query_weight.shape[2]
    kv_width = key_weight.shape[2]
    all_queries = query_width * col_count
    all_kv = kv_width * col_count
    head_scale = HEAD ** (-0.5)

    deal = []
    for j in range(row_count):
        deal += [j, 2 * row_count - 1 - j]
    undeal = [deal.index(b) for b in range(2 * row_count)]

    def reorder(values, order):
        parts = [values[..., b * half_block : (b + 1) * half_block] for b in order]
        return jnp.concatenate(parts, -1)

    def to_token_blocks(values):
        chunks = spread(reorder(values, deal), row_count)
        return rows_exchange(chunks, row_index).reshape(-1, block_tokens).T

    def to_feature_blocks(values):
        chunks = values.astype(LOW).T.reshape(row_count, feat_width, block_tokens)
        return reorder(unspread(rows_exchange(chunks, row_index)), undeal).astype(jnp.float32)

    def blocks_here(values):
        dealt = reorder(values, deal).reshape(row_count, block_tokens)
        picked = [
            lax.dynamic_index_in_dim(dealt, row_index ^ i, 0, keepdims=False)
            for i in range(row_count)
        ]
        return jnp.concatenate(picked)

    places = blocks_here(jnp.arange(col_tokens, dtype=jnp.int32))
    own_positions = blocks_here(
        lax.dynamic_index_in_dim(positions, col_index, 0, keepdims=False)
    )[:block_tokens]
    doc = blocks_here(lax.dynamic_index_in_dim(segments, col_index, 0, keepdims=False))
    allowed = (places[:, None] <= places[None, :block_tokens]) & (
        doc[:, None] == doc[None, :block_tokens]
    )
    bias = jnp.where(allowed, 0.0, NEG_FILL)
    cosine, sine = rope_tables(own_positions)

    def attention_wide(layer, earlier=None):
        joint = jnp.concatenate(
            [query_weight[layer], key_weight[layer], value_weight[layer], out_weight[layer].T], 1
        )
        if earlier is not None:
            joint = after(joint, earlier)
        wide = lax.all_gather(joint, "cols", axis=0, tiled=True)
        wide = wide.reshape(col_count, feat_width, -1)
        ends = [query_width, query_width + kv_width, query_width + 2 * kv_width]
        parts = [unspread(part) for part in jnp.split(wide, ends, 2)]
        return jnp.concatenate(parts[:3], 1), parts[3]

    def attention_weights(wides, earlier, first):
        joint_wide, out_wide = wides
        joint_wide = after(joint_wide, earlier)
        if first:
            joint_full = relabel(rows_gather(joint_wide), row_index)
            out_full = relabel(rows_gather(out_wide), row_index)
            return joint_full, out_full
        joint_full = lax.all_gather(joint_wide, "rows", axis=0, tiled=True)
        out_full = lax.all_gather(out_wide, "rows", axis=0, tiled=True)
        return joint_full, out_full

    def ffn_shard(layer):
        stacked = jnp.stack([gate_weight[layer], up_weight[layer], down_weight[layer]])
        chunks = stacked.transpose(0, 2, 1).reshape(3, row_count, 2, -1, feat_width)
        half = lax.dynamic_index_in_dim(chunks, dp_index % 2, 2, keepdims=False)
        whole = rows_exchange(half.transpose(1, 0, 2, 3), row_index)
        return whole.transpose(1, 2, 0, 3).reshape(-1, row_count * feat_width)

    def ffn_weights(own):
        other = swap_dp(own, 1)
        own = own.reshape(col_count, 3, -1, row_count * feat_width)
        other = other.reshape(own.shape)
        return [
            jnp.concatenate([own[:, i], other[:, i]], 0).reshape(-1, row_count * feat_width)
            for i in range(3)
        ]

    def attention_parts(joint_grad, out_grad, last):
        low = joint_grad.astype(LOW)
        if last:
            part = rows_scatter(relabel(low, row_index)).astype(LOW)
        else:
            part = lax.psum_scatter(low, "rows", scatter_dimension=0, tiled=True)
        out = lax.psum_scatter(out_grad.astype(LOW), "rows", scatter_dimension=0, tiled=True)
        ends = [all_queries, all_queries + all_kv]
        parts = [spread(p, col_count) for p in jnp.split(part, ends, 1) + [out]]
        return jnp.concatenate(parts, 2).reshape(col_count * feat_width, -1)

    def attention_grads(joint):
        joint = lax.psum_scatter(joint, "cols", scatter_dimension=0, tiled=True)
        step = 1
        while step < dp_count:
            joint = joint.astype(jnp.float32) + swap_dp(joint.astype(LOW), step).astype(jnp.float32)
            step *= 2
        ends = [query_width, query_width + kv_width, query_width + 2 * kv_width]
        parts = jnp.split(joint, ends, 1)
        return parts[0], parts[1], parts[2], parts[3].T

    def ffn_grads(grads, earlier):
        stacked = jnp.stack([g.astype(LOW).reshape(2, col_count, -1, g.shape[1]) for g in grads], 2)
        other = after(swap_dp(stacked[1], 1), earlier)
        half = stacked[0].astype(jnp.float32) + other.astype(jnp.float32)
        half = half.astype(LOW).reshape(-1, half.shape[-1])
        mine = lax.psum_scatter(half, "cols", scatter_dimension=0, tiled=True)
        step = 2
        while step < dp_count:
            mine = (mine.astype(jnp.float32) + swap_dp(mine, step).astype(jnp.float32)).astype(LOW)
            step *= 2
        chunks = mine.reshape(3, -1, row_count, feat_width).transpose(2, 0, 1, 3)
        mine = rows_exchange(chunks, row_index)
        other = swap_dp(mine, 1)
        first = dp_index % 2 == 0
        both = jnp.stack([jnp.where(first, mine, other), jnp.where(first, other, mine)], 2)
        both = both.transpose(1, 4, 0, 2, 3)
        return both.reshape(3, feat_width, -1).astype(jnp.float32)

    def everywhere(value):
        for axis in ("rows", "dp", "cols"):
            count = lax.axis_size(axis)
            step = 1
            while step < count:
                value = value + lax.ppermute(value, axis, [(i, i ^ step) for i in range(count)])
                step *= 2
        return value

    shards = [ffn_shard(n) for n in range(layer_total)]
    attention_ws = [attention_weights(attention_wide(0), shards[0], True)]
    ffn_own = [lax.all_gather(shards[0], "cols", axis=0, tiled=True)]
    ffn_ws = []

    residual = to_token_blocks(tokens).astype(jnp.float32)
    saved = []
    for layer in range(layer_total):
        joint_full, out_full = attention_ws[layer]
        normed, mixer_scale = norm_forward(residual, attention_gain[layer])
        projected = contract(joint_full, normed, 0, 1).astype(LOW).astype(jnp.float32)
        queries = (turn(projected[:all_queries], cosine, sine) * head_scale).astype(LOW)
        own_kv = jnp.concatenate(
            [
                turn(projected[all_queries : all_queries + all_kv], cosine, sine),
                projected[all_queries + all_kv :],
            ],
            0,
        ).astype(LOW)
        both = rows_gather(own_kv).reshape(row_count, 2 * all_kv, block_tokens)
        mixed, log_norm = attend_forward(queries, both, bias)
        own_shards = after(ffn_own[layer], both if layer else mixed)
        ffn_ws.append(ffn_weights(own_shards))
        gate_full, up_full, down_full = ffn_ws[layer]
        hidden = residual + contract(mixed, out_full, 0, 1)
        ffn_normed, ffn_scale = norm_forward(hidden, feedforward_gain[layer])
        ffn_all = rows_gather(ffn_normed)
        gate = contract(ffn_all, gate_full, 1, 1)
        up = contract(ffn_all, up_full, 1, 1)
        if layer + 1 < layer_total:
            wides = attention_wide(layer + 1, own_shards)
            attention_ws.append(attention_weights(wides, gate, False))
            shard = after(shards[layer + 1], gate)
            ffn_own.append(lax.all_gather(shard, "cols", axis=0, tiled=True))
        activated = (gate * jax.nn.sigmoid(gate) * up).astype(LOW)
        ffn_out = rows_scatter(contract(activated, down_full, 1, 0))
        saved.append(
            (residual, mixer_scale, normed, queries, both, log_norm, mixed, hidden)
            + (ffn_scale, ffn_all, gate, up, activated)
        )
        residual = hidden + ffn_out

    weight_grads = [None] * layer_total
    gain_grads = [None] * layer_total
    waiting = None
    grad = to_token_blocks(cotangent).astype(jnp.float32)
    for layer in reversed(range(layer_total)):
        joint_full, out_full = attention_ws[layer]
        gate_full, up_full, down_full = ffn_ws[layer]
        layer_input, mixer_scale, normed, queries, both, log_norm, mixed, hidden = saved[layer][:8]
        ffn_scale, ffn_all, gate, up, activated = saved[layer][8:]
        grad_all = rows_gather(grad.astype(LOW))
        grad_act = contract(grad_all, down_full, 1, 1)
        down_grad = contract(activated, grad_all, 0, 0)
        sig = jax.nn.sigmoid(gate)
        grad_gate = (grad_act * up * sig * (1.0 + gate * (1.0 - sig))).astype(LOW)
        grad_up = (grad_act * gate * sig).astype(LOW)
        grad_ffn_normed = rows_scatter(
            contract(grad_gate, gate_full, 1, 0) + contract(grad_up, up_full, 1, 0)
        )
        gate_grad = contract(grad_gate, ffn_all, 0, 0)
        up_grad = contract(grad_up, ffn_all, 0, 0)
        ffn_norm_grad, ffn_gain_grad = norm_backward(
            grad_ffn_normed, hidden, ffn_scale, feedforward_gain[layer]
        )
        grad_hidden = grad + ffn_norm_grad
        grad_low = grad_hidden.astype(LOW)
        grad_mixed = contract(out_full, grad_low, 0, 1).astype(LOW)
        out_grad = contract(grad_low, mixed, 0, 1)
        if waiting is not None:
            grad_mixed = after(grad_mixed, waiting)
        grad_query, grad_key, grad_value = attend_backward(
            queries, both, bias, mixed, log_norm, grad_mixed
        )
        grad_kv = jnp.concatenate([grad_key, grad_value], 1).reshape(-1, block_tokens)
        grad_kv = rows_scatter(grad_kv)
        grad_joint = jnp.concatenate(
            [
                turn(grad_query, cosine, -sine) * head_scale,
                turn(grad_kv[:all_kv], cosine, -sine),
                grad_kv[all_kv:],
            ],
            0,
        ).astype(LOW)
        grad_normed = contract(grad_joint, joint_full, 0, 1)
        joint_grad = contract(normed, grad_joint, 0, 1)
        mixer_norm_grad, mixer_gain_grad = norm_backward(
            grad_normed, layer_input, mixer_scale, attention_gain[layer]
        )
        grad = grad_hidden + mixer_norm_grad
        ffn_parts = ffn_grads([gate_grad, up_grad, down_grad], grad_query)
        waiting = attention_parts(joint_grad, out_grad, layer == 0)
        weight_grads[layer] = attention_grads(waiting) + (
            ffn_parts[0],
            ffn_parts[1],
            ffn_parts[2],
        )
        gain_grads[layer] = jnp.stack([mixer_gain_grad, ffn_gain_grad])

    gain_total = everywhere(jnp.stack(gain_grads))
    totals = [jnp.stack([weight_grads[n][i] for n in range(layer_total)]) for i in range(7)]
    return (
        to_feature_blocks(residual),
        to_feature_blocks(grad),
        totals[0],
        totals[1],
        totals[2],
        totals[3],
        totals[4],
        totals[5],
        totals[6],
        gain_total[:, 0],
        gain_total[:, 1],
    )


def solution(mesh):
    whole = P("rows", ("dp", "cols"))
    weight = P(None, "rows", "cols")
    flipped = P(None, "cols", "rows")
    return jax.shard_map(
        on_device,
        mesh=mesh,
        in_specs=(whole, weight, weight, weight, flipped, weight, weight, weight)
        + (P(), P(), P("dp", None), P("dp", None), whole),
        out_specs=(whole, whole, weight, weight, weight, flipped, weight, weight, weight, P(), P()),
        check_vma=False,
    )
```
